32 devices in a mesh: section: 8 (over z, y), expert: 4 (over x, core).
Axes of the slice: x: 2, y: 2, z: 4, core: 2. Of those that a mesh axis runs over, the one named last changes fastest.
Arguments:
- carried: bfloat16 [8, 512, 2048], P('section', 'expert'), may hold values from -6 to 6
- saved_rows: bfloat16 [8, 512, 2048], P('section', 'expert'), may hold values from -6 to 6
- returned: bfloat16 [8, 512, 2048], P('section', 'expert'), may hold values from -6 to 6
- fwd_ids: int32 [8, 512, 2], P('section', 'expert'), may hold values from 0 to 3, all different within a row; in each aligned block of 128 rows (0 to 127, 128 to 255, ..., all dimensions but the last counted through in order) at most 72 rows name the same one
- fwd_gates: float32 [8, 512, 2], P('section', 'expert'), may hold values from 0.2 to 1
- bwd_ids: int32 [8, 512, 2], P('section', 'expert'), may hold values from 0 to 3, all different within a row; in each aligned block of 128 rows (0 to 127, 128 to 255, ..., all dimensions but the last counted through in order) at most 72 rows name the same one
- bwd_gates: float32 [8, 512, 2], P('section', 'expert'), may hold values from 0.2 to 1
- gate_w: bfloat16 [8, 2048, 4096], P('section', None, 'expert'), may hold values from -0.125 to 0.125
- up_w: bfloat16 [8, 2048, 4096], P('section', None, 'expert'), may hold values from -0.125 to 0.125
- down_w: bfloat16 [8, 4096, 2048], P('section', 'expert'), may hold values from -0.1875 to 0.1875
Outputs:
- next_input: bfloat16 [8, 512, 2048], P('section', 'expert')
- grad_input: bfloat16 [8, 512, 2048], P('section', 'expert')
- gate_grad: float32 [8, 2048, 4096], P('section', None, 'expert')
- up_grad: float32 [8, 2048, 4096], P('section', None, 'expert')
- down_grad: float32 [8, 4096, 2048], P('section', 'expert')
The draws below stay inside these ranges and needn't reach their ends.
Inputs may be any that keep to these rules, and one draw needn't show every extreme that they name: `fwd_ids`: the 2 ids of a token differ. In each aligned block of 128 tokens (one device's tokens of one section) each expert is named by at most 72 tokens, a bound that some block reaches. `bwd_ids`: the 2 ids of a token differ. In each aligned block of 128 tokens each expert is named by at most 72 tokens, a bound that some block reaches.
All inputs are finite; a program needn't handle non-finite values.
Results may differ from the reference program's by a relative error of at most 0.0052.
Values may be sent and summed in bfloat16 or wider, within the bound.
No kernel may reach another device: no remote copies, remote signals or barrier semaphores. Data moves between devices by JAX's collectives and lax.ppermute only.
A program may use at most 128 MiB of HBM per device.

```python
import math
import jax
import jax.numpy as jnp
import numpy as np
from jax import lax

D = 2048
H_WIN = 1024
E_WIN = 4
TOP = 2
TOK_DEV = 128
CAP = 72
SECTIONS = 8
TOKENS = 512
N_EXPERT = 4


def block_scale(stream_key, shape, split, low, high):
    loudness, own = 1.0, jax.random.fold_in(stream_key, 6)
    for position, parts in split:
        steps = jnp.exp(jax.random.uniform(jax.random.fold_in(own, position), (parts,), jnp.float32, low / len(split), high / len(split)))
        loudness = loudness * jnp.repeat(steps, shape[position] // parts).reshape([-1 if axis == position else 1 for axis in range(len(shape))])
    return loudness


def assign_block(own_key, own, number, rows, number_of, top, reach, skew):
    ranking = jax.random.permutation(own_key, number_of)
    crowded, usual = shares(number_of, rows * top, reach, skew, True), shares(number_of, rows * top, reach, skew, False)
    places = jnp.arange(number_of)

    def named(sizes, offset_by):
        used = int((sizes > 0).sum())
        fixed = max(1, used // 4)
        passed = fixed + (places - fixed + offset_by * (used - fixed)) % max(1, number_of - fixed)
        return jnp.zeros((number_of,), jnp.int32).at[ranking[jnp.where(places < fixed, places, passed)]].set(jnp.asarray(sizes, jnp.int32))

    sizes = jnp.where(number % 4 == 0, named(crowded, number // 4), named(usual, number - number // 4 - 1))
    mixed = jax.random.permutation(jax.random.fold_in(own, 3), number_of)
    source_of, receiver = mixed[0:number_of // 2 * 2:2], mixed[1:number_of // 2 * 2:2]
    room = jnp.minimum(sizes[source_of] - 1, reach - sizes[receiver]) // 2
    room = jnp.where((source_of == ranking[0]) | (receiver == ranking[0]) | (sizes[receiver] == 0), 0, jnp.maximum(room, 0))
    passed = jax.random.randint(jax.random.fold_in(own, 4), (number_of // 2,), 0, 1 << 20) % (room + 1)
    sizes = sizes.at[source_of].add(-passed).at[receiver].add(passed)
    items = jnp.searchsorted(jnp.cumsum(sizes), jnp.arange(rows * top), side="right").astype(jnp.int32)
    listing = items.reshape(top, rows).T
    listing = listing[jax.random.permutation(jax.random.fold_in(own, 1), rows)]
    offset_by = jax.random.randint(jax.random.fold_in(own, 2), (rows, 1), 0, top)
    return jnp.take_along_axis(listing, (jnp.arange(top)[None, :] + offset_by) % top, axis=1)


def shares(count, total, reach, slope, full):
    loads = [(1 << 20) // math.isqrt(grade ** slope) + 1 for grade in range(1, count + 1)]
    largest = reach if full else min(reach, max(-(-total // count), total * loads[0] // sum(loads)))
    least = 1 if total - largest >= count - 1 else 0
    holding, rest = [largest] + [least] * (count - 1), total - largest - least * (count - 1)
    while rest > 0:
        movable = [i for i in range(1, count) if holding[i] < largest] or [i for i in range(1, count) if holding[i] < reach]
        mass, remaining = sum([loads[i] for i in movable]), rest
        for i in movable:
            more = min(reach - holding[i], max(1, remaining * loads[i] // mass), rest)
            holding[i] = holding[i] + more
            rest = rest - more
    return np.array(holding)


def scatter_about(key, shape, width, most, split=(), dtype=jnp.bfloat16):
    values = width * jax.random.normal(key, shape, jnp.float32)
    if split:
        values = values * block_scale(key, shape, split, -0.22, 0.18)
    return jnp.clip(values, -most, most).astype(dtype)


def setup_inputs(seed: int = 0) -> dict:
    splits = jax.random.split(jax.random.key(seed), 11)
    carried = scatter_about(splits[0], (SECTIONS, TOKENS, D), 1.0, 6.0, ((0, 8), (1, 4)))
    saved_rows = scatter_about(splits[1], (SECTIONS, TOKENS, D), 1.0, 6.0, ((0, 8), (1, 4)))
    returned = scatter_about(splits[2], (SECTIONS, TOKENS, D), 1.0, 6.0, ((0, 8), (1, 4)))
    fwd_ids_keys = jax.random.split(jax.random.fold_in(splits[3], 1), SECTIONS * TOKENS // TOK_DEV)
    fwd_ids_turns = jax.random.permutation(jax.random.fold_in(splits[3], 3), SECTIONS * TOKENS // TOK_DEV)
    fwd_ids = jax.vmap(lambda own, number: assign_block(jax.random.fold_in(splits[3], 2), own, number, TOK_DEV, E_WIN, TOP, CAP, 2))(fwd_ids_keys, fwd_ids_turns).reshape((SECTIONS, TOKENS, TOP))
    fwd_gates = jnp.clip(jnp.exp(math.log(1.0) - 1.609438 * jax.random.uniform(splits[4], (SECTIONS, TOKENS, TOP), jnp.float32) ** block_scale(splits[4], (SECTIONS, TOKENS, TOP), ((0, 8), (1, 4)), -0.2, 0.2)), 0.2, 1.0)
    bwd_ids_keys = jax.random.split(jax.random.fold_in(splits[5], 1), SECTIONS * TOKENS // TOK_DEV)
    bwd_ids_turns = jax.random.permutation(jax.random.fold_in(splits[5], 3), SECTIONS * TOKENS // TOK_DEV)
    bwd_ids = jax.vmap(lambda own, number: assign_block(jax.random.fold_in(splits[5], 2), own, number, TOK_DEV, E_WIN, TOP, CAP, 2))(bwd_ids_keys, bwd_ids_turns).reshape((SECTIONS, TOKENS, TOP))
    bwd_gates = jnp.clip(jnp.exp(math.log(1.0) - 1.609438 * jax.random.uniform(splits[6], (SECTIONS, TOKENS, TOP), jnp.float32) ** block_scale(splits[6], (SECTIONS, TOKENS, TOP), ((0, 8), (1, 4)), -0.2, 0.2)), 0.2, 1.0)
    gate_w = scatter_about(splits[7], (SECTIONS, D, E_WIN * H_WIN), D ** -0.5, 0.125, ((0, 8), (2, 4)))
    up_w = scatter_about(splits[8], (SECTIONS, D, E_WIN * H_WIN), D ** -0.5, 0.125, ((0, 8), (2, 4)))
    down_w = scatter_about(splits[9], (SECTIONS, E_WIN * H_WIN, D), H_WIN ** -0.5, 0.1875, ((0, 8), (1, 4)))
    return {"carried": carried, "saved_rows": saved_rows, "returned": returned, "fwd_ids": fwd_ids, "fwd_gates": fwd_gates, "bwd_ids": bwd_ids, "bwd_gates": bwd_gates, "gate_w": gate_w, "up_w": up_w, "down_w": down_w}


def expert_order(route_ids, route_gates, expert):
    hit = route_ids == expert
    share = jnp.sum(jnp.where(hit, route_gates, jnp.zeros_like(route_gates)), axis=1)
    chosen = jnp.any(hit, axis=1)
    keyed = jnp.where(chosen, 0, 1).astype(jnp.int32)
    order = jnp.argsort(keyed, stable=True)[: N_EXPERT * CAP].astype(jnp.int32)
    return order, share[order]


def section_pass(packed):
    layer_in, fwd_route, fwd_weight, saved_in, bwd_route, bwd_weight, cotangent, gate_mat, up_mat, down_mat = packed
    group_size = N_EXPERT // E_WIN
    slice_width = H_WIN // group_size
    output_sum = layer_in.astype(jnp.float32)
    input_grad = cotangent.astype(jnp.float32)
    gate_cols = []
    up_cols = []
    down_rows = []
    for expert in range(E_WIN):
        first = expert * H_WIN
        gate_part = gate_mat[:, first:first + H_WIN]
        up_part = up_mat[:, first:first + H_WIN]
        down_part = down_mat[first:first + H_WIN, :]
        order, share = expert_order(fwd_route, fwd_weight, expert)
        token_rows = layer_in[order]
        pre_gate = jnp.dot(token_rows, gate_part, preferred_element_type=jnp.float32)
        pre_up = jnp.dot(token_rows, up_part, preferred_element_type=jnp.float32)
        sigma = jax.nn.sigmoid(pre_gate)
        hidden = (pre_gate * sigma * pre_up).astype(jnp.bfloat16)
        expert_out = jnp.zeros((token_rows.shape[0], D), jnp.float32)
        for piece in range(group_size):
            low = piece * slice_width
            term = jnp.dot(hidden[:, low:low + slice_width], down_part[low:low + slice_width], preferred_element_type=jnp.float32).astype(jnp.bfloat16)
            expert_out = expert_out + lax.optimization_barrier(term).astype(jnp.float32)
        output_sum = output_sum.at[order].add(share[:, None] * expert_out)
        order_b, share_b = expert_order(bwd_route, bwd_weight, expert)
        saved = saved_in[order_b]
        scaled = (share_b[:, None] * cotangent[order_b].astype(jnp.float32)).astype(jnp.bfloat16)
        pre_gate2 = jnp.dot(saved, gate_part, preferred_element_type=jnp.float32)
        pre_up2 = jnp.dot(saved, up_part, preferred_element_type=jnp.float32)
        sigma2 = jax.nn.sigmoid(pre_gate2)
        swish = pre_gate2 * sigma2
        hidden2 = (swish * pre_up2).astype(jnp.bfloat16)
        grad_hidden = jnp.dot(scaled, down_part.T, preferred_element_type=jnp.float32)
        grad_gate_pre = (grad_hidden * pre_up2 * sigma2 * (1.0 + pre_gate2 * (1.0 - sigma2))).astype(jnp.bfloat16)
        grad_up_pre = (grad_hidden * swish).astype(jnp.bfloat16)
        back_sum = jnp.zeros((saved.shape[0], D), jnp.float32)
        for piece in range(group_size):
            low = piece * slice_width
            high = low + slice_width
            term = jnp.dot(grad_gate_pre[:, low:high], gate_part[:, low:high].T, preferred_element_type=jnp.float32)
            term = term + jnp.dot(grad_up_pre[:, low:high], up_part[:, low:high].T, preferred_element_type=jnp.float32)
            term = term.astype(jnp.bfloat16)
            back_sum = back_sum + lax.optimization_barrier(term).astype(jnp.float32)
        input_grad = input_grad.at[order_b].add(back_sum)
        gate_cols.append(jnp.dot(saved.T, grad_gate_pre, preferred_element_type=jnp.float32))
        up_cols.append(jnp.dot(saved.T, grad_up_pre, preferred_element_type=jnp.float32))
        down_rows.append(jnp.dot(hidden2.T, scaled, preferred_element_type=jnp.float32))
    return (output_sum.astype(jnp.bfloat16), input_grad.astype(jnp.bfloat16), jnp.concatenate(gate_cols, axis=1), jnp.concatenate(up_cols, axis=1), jnp.concatenate(down_rows, axis=0))


def reference(carried, saved_rows, returned, fwd_ids, fwd_gates, bwd_ids, bwd_gates, gate_w, up_w, down_w):
    arrived = jnp.roll(carried, 1, axis=0)
    incoming = jnp.roll(returned, -1, axis=0)
    results = lax.map(section_pass, (arrived, fwd_ids, fwd_gates, saved_rows, bwd_ids, bwd_gates, incoming, gate_w, up_w, down_w))
    return (results[0], results[1], results[2], results[3], results[4])
```

```python
import jax
import jax.numpy as jnp
from jax import lax
from jax.sharding import PartitionSpec as P

E_WIN = 4
CAP = 72


def passed_along(value, steps):
    count = lax.axis_size("section")
    pairs = [(source, (source + steps) % count) for source in range(count)]
    return lax.ppermute(value, "section", pairs)


def swapped(value, bit):
    count = lax.axis_size("expert")
    return lax.ppermute(value, "expert", [(source, source ^ bit) for source in range(count)])


def bits_of(count):
    bits = []
    while count > 1:
        count //= 2
        bits.append(count)
    return bits


def gathered(value):
    buffer = value[None]
    for bit in bits_of(lax.axis_size("expert")):
        buffer = jnp.concatenate([buffer, swapped(buffer, bit)], axis=0)
    return buffer


def returned_sum(partials):
    bits = bits_of(lax.axis_size("expert"))[::-1]
    for step, bit in enumerate(bits):
        half = partials.shape[0] // 2
        total = partials[:half].astype(jnp.float32) + swapped(partials[half:], bit).astype(jnp.float32)
        partials = total if step == len(bits) - 1 else total.astype(jnp.bfloat16)
    return partials[0]


def routing(ids, gates, expert):
    hit = ids == expert.astype(jnp.float32)
    share = jnp.sum(jnp.where(hit, gates, 0.0), axis=1)
    chosen = jnp.any(hit, axis=1)
    rows = ids.shape[2]
    earlier = (jnp.arange(rows)[:, None] < jnp.arange(rows)[None, :]).astype(jnp.bfloat16)
    rank = jnp.dot(chosen.astype(jnp.bfloat16), earlier, preferred_element_type=jnp.float32)
    rank = jnp.where(chosen, rank, -1.0)
    slots = jnp.arange(CAP, dtype=jnp.int32).astype(jnp.float32)
    match = rank[:, None, :] == slots[None, :, None]
    slot_gate = jnp.sum(jnp.where(match, share[:, None, :], 0.0), axis=2)
    return match.astype(jnp.bfloat16), slot_gate.reshape(-1, 1)


def picked(table, rows):
    out = jnp.einsum("bct,btd->bcd", table, rows, preferred_element_type=jnp.float32)
    return out.astype(jnp.bfloat16).reshape(-1, rows.shape[-1])


def placed_back(table, values):
    values = values.astype(jnp.bfloat16).reshape(table.shape[0], CAP, values.shape[-1])
    out = jnp.einsum("bct,bcd->btd", table, values, preferred_element_type=jnp.float32)
    return out.astype(jnp.bfloat16)


def body(
    carried, saved_rows, returned, fwd_ids, fwd_gates, bwd_ids, bwd_gates, gate_w, up_w, down_w
):
    devices = lax.axis_size("expert")
    group_size = devices // E_WIN
    expert = lax.axis_index("expert") // group_size
    gate_part = gate_w[0]
    up_part = up_w[0]
    down_part = down_w[0]
    routes = jnp.concatenate(
        [
            fwd_ids[0].T.astype(jnp.float32),
            bwd_ids[0].T.astype(jnp.float32),
            fwd_gates[0].T,
            bwd_gates[0].T,
        ],
        axis=0,
    )
    saved_all = gathered(saved_rows[0])
    cotangent = passed_along(returned, -1)[0]
    layer_in = passed_along(carried, 1)[0]
    routes = gathered(routes)
    fwd_table, fwd_slot_gate = routing(routes[:, 0:2], routes[:, 4:6], expert)
    bwd_table, bwd_slot_gate = routing(routes[:, 2:4], routes[:, 6:8], expert)

    saved = picked(bwd_table, saved_all)
    pre_gate2 = jnp.dot(saved, gate_part, preferred_element_type=jnp.float32)
    pre_up2 = jnp.dot(saved, up_part, preferred_element_type=jnp.float32)
    sigma2 = jax.nn.sigmoid(pre_gate2)
    swish = pre_gate2 * sigma2
    hidden2 = (swish * pre_up2).astype(jnp.bfloat16)

    chosen_grads = picked(bwd_table, gathered(cotangent))
    scaled = (bwd_slot_gate * chosen_grads.astype(jnp.float32)).astype(jnp.bfloat16)
    grad_hidden = jnp.einsum("rd,hd->rh", scaled, down_part, preferred_element_type=jnp.float32)
    grad_gate_pre = (grad_hidden * pre_up2 * sigma2 * (1.0 + pre_gate2 * (1.0 - sigma2))).astype(
        jnp.bfloat16
    )
    grad_up_pre = (grad_hidden * swish).astype(jnp.bfloat16)
    back = jnp.einsum("rh,dh->rd", grad_gate_pre, gate_part, preferred_element_type=jnp.float32)
    back = back + jnp.einsum("rh,dh->rd", grad_up_pre, up_part, preferred_element_type=jnp.float32)
    input_grad = cotangent.astype(jnp.float32) + returned_sum(placed_back(bwd_table, back))

    token_rows = picked(fwd_table, gathered(layer_in))
    pre_gate = jnp.dot(token_rows, gate_part, preferred_element_type=jnp.float32)
    pre_up = jnp.dot(token_rows, up_part, preferred_element_type=jnp.float32)
    hidden = (pre_gate * jax.nn.sigmoid(pre_gate) * pre_up).astype(jnp.bfloat16)
    expert_out = fwd_slot_gate * jnp.dot(hidden, down_part, preferred_element_type=jnp.float32)
    output_sum = layer_in.astype(jnp.float32) + returned_sum(placed_back(fwd_table, expert_out))

    down_grad = jnp.einsum("rh,rd->hd", hidden2, scaled, preferred_element_type=jnp.float32)
    gate_grad = jnp.einsum("rd,rh->dh", saved, grad_gate_pre, preferred_element_type=jnp.float32)
    up_grad = jnp.einsum("rd,rh->dh", saved, grad_up_pre, preferred_element_type=jnp.float32)
    return (
        output_sum.astype(jnp.bfloat16)[None],
        input_grad.astype(jnp.bfloat16)[None],
        gate_grad[None],
        up_grad[None],
        down_grad[None],
    )


def solution(mesh):
    rows = P("section", "expert", None)
    columns = P("section", None, "expert")
    return jax.shard_map(
        body,
        mesh=mesh,
        in_specs=(rows, rows, rows, rows, rows, rows, rows, columns, columns, rows),
        out_specs=(rows, rows, columns, columns, rows),
        check_vma=False,
    )
```
